32 devices in a mesh: rep: 2 (over x), ctx: 8 (over z, y), tp: 2 (over core).
Axes of the slice: x: 2, y: 2, z: 4, core: 2. Of those that a mesh axis runs over, the one named last changes fastest.
Arguments:
- queries: bfloat16 [4096, 4096], P(('rep', 'ctx'), 'tp'), parts along dimension 0, may hold values from -8 to 8
- rotated_key_rows: bfloat16 [4096, 512], P(('rep', 'ctx'), 'tp'), parts along dimension 0, may hold values from -8 to 8
- ordered_value_rows: bfloat16 [4096, 512], P(('rep', 'ctx'), 'tp'), parts along dimension 0, may hold values from -6 to 6
- block_order: int32 [32], P('rep'), parts along dimension 0, may hold values from 0 to 15, each once
- live_blocks: int32 [32, 12], P('rep'), parts along dimension 0, may hold values from -1 to 15, as said below
Outputs:
- attended: bfloat16 [4096, 4096], P(('rep', 'ctx', 'tp')), parts along dimension 0
- log_norm: float32 [64, 2048], P(('rep', 'tp'), 'ctx'), parts along dimension 0
The draws below stay inside these ranges and needn't reach their ends.
There are 2 independent parts, one for each index of `rep`. The reference program is written for one: setup_inputs(seed, part) draws one part's arguments, and reference() takes and returns one part's arrays. A program takes and returns all parts, laid end to end along the dimension named above; each array names one. Nothing has to cross between parts.
Inputs may be any that keep to these rules, and one draw needn't show every extreme that they name: `live_blocks`: row s names block s in its first slot, then distinct blocks before s, then -1 in every unused slot; row 15 fills all 12 slots.
All inputs are finite; a program needn't handle non-finite values.
Results may differ from the reference program's by a relative error of at most 0.008.
Values may be sent and summed in bfloat16 or wider, within the bound.
A program may use at most 128 MiB of HBM per device.

```python
import jax
import jax.numpy as jnp
from jax import lax

QUERY_HEADS = 32
KEY_VALUE_HEADS = 4
HEAD_SIZE = 128
BLOCK_TOKENS = 128
PROMPT_TOKENS = 2048
PROMPT_BLOCKS = 16
LIVE = 12


def base_random_field(key, shape):
    return jnp.clip(jax.random.normal(key, shape, jnp.float32), -8.0, 8.0)


def draw_queries(key, part):
    sampled_field = base_random_field(jax.random.fold_in(key, 1), (PROMPT_TOKENS, QUERY_HEADS * HEAD_SIZE))
    return sampled_field.astype(jnp.bfloat16)


def draw_rotated_key_rows(key, part):
    sampled_field = base_random_field(jax.random.fold_in(key, 2), (PROMPT_TOKENS, KEY_VALUE_HEADS * HEAD_SIZE))
    return sampled_field.astype(jnp.bfloat16)


def draw_live_blocks(key, part):
    first_key = jax.random.fold_in(key, 11)
    second_key = jax.random.fold_in(key, 12)
    row_ids = jnp.arange(PROMPT_BLOCKS, dtype=jnp.int32)
    uniform_pick = jax.random.randint(first_key, (PROMPT_BLOCKS,), 0, LIVE)
    wanted = LIVE - uniform_pick * uniform_pick // LIVE
    live_count = jnp.minimum(row_ids + 1, wanted)
    live_count = live_count.at[PROMPT_BLOCKS - 1].set(LIVE)
    col_ids = jnp.arange(PROMPT_BLOCKS, dtype=jnp.int32)
    ranked = jax.random.randint(second_key, (PROMPT_BLOCKS, PROMPT_BLOCKS), 0, 1 << 20) * PROMPT_BLOCKS + col_ids[None, :]
    ranked = jnp.where(col_ids[None, :] < row_ids[:, None], ranked, -1)
    top_values, earlier = jax.lax.top_k(ranked, LIVE - 1)
    slot_ids = jnp.arange(LIVE - 1, dtype=jnp.int32)
    entries = jnp.where(slot_ids[None, :] < live_count[:, None] - 1, earlier.astype(jnp.int32), -1)
    return jnp.concatenate([row_ids[:, None], entries], axis=1)


def block_levels(rng, dims, cuts, least, high):
    level = 1.0
    for dim, blocks in cuts:
        draws = jax.random.uniform(jax.random.fold_in(jax.random.fold_in(rng, 6), dim), (blocks,), jnp.float32, least / len(cuts), high / len(cuts))
        level = level * jnp.repeat(jnp.exp(draws), dims[dim] // blocks).reshape((-1,) + (1,) * (len(dims) - 1 - dim))
    return level


def scatter_about(stream_key, extent, deviation, reach, pieces=(), held_as=jnp.bfloat16):
    drawn = jax.random.normal(stream_key, extent, jnp.float32) * deviation
    if len(pieces) > 0:
        drawn = block_levels(stream_key, extent, pieces, -0.22, 0.18) * drawn
    return jnp.clip(drawn, min=-reach, max=reach).astype(held_as)


def setup_inputs(seed: int = 0, part: int = 0) -> dict:
    seeds = jax.random.split(jax.random.key(seed), 6)
    own_keys = jax.random.split(jax.random.fold_in(seeds[5], part), 6)
    return {
        "queries": draw_queries(jax.random.fold_in(jax.random.fold_in(seeds[5], part), 71), part),
        "rotated_key_rows": draw_rotated_key_rows(jax.random.fold_in(jax.random.fold_in(seeds[5], part), 71), part),
        "ordered_value_rows": scatter_about(own_keys[2], (PROMPT_TOKENS, KEY_VALUE_HEADS * HEAD_SIZE), 1.0, 6.0, ((0, 8), (1, 2))),
        "block_order": jax.random.permutation(own_keys[3], PROMPT_BLOCKS).astype(jnp.int32),
        "live_blocks": draw_live_blocks(jax.random.fold_in(jax.random.fold_in(seeds[5], part), 71), part),
    }


def reference(queries, rotated_key_rows, ordered_value_rows, block_order, live_blocks):
    query_groups = QUERY_HEADS // KEY_VALUE_HEADS
    factor = HEAD_SIZE ** -0.5
    block_ids = jnp.arange(PROMPT_BLOCKS, dtype=jnp.int32)
    inverse = jnp.zeros((PROMPT_BLOCKS,), jnp.int32).at[block_order].set(block_ids)
    blocked_keys = rotated_key_rows.reshape(PROMPT_BLOCKS, BLOCK_TOKENS, KEY_VALUE_HEADS, HEAD_SIZE)
    blocked_values = ordered_value_rows.reshape(PROMPT_BLOCKS, BLOCK_TOKENS, KEY_VALUE_HEADS, HEAD_SIZE)
    blocked_queries = queries.reshape(PROMPT_BLOCKS, BLOCK_TOKENS, KEY_VALUE_HEADS, query_groups, HEAD_SIZE)
    within = jnp.arange(BLOCK_TOKENS, dtype=jnp.int32)

    def one_block(index):
        seq_id = block_order[index]
        listed = live_blocks[seq_id]
        in_use = listed >= 0
        places = inverse[jnp.maximum(listed, 0)]
        picked_keys = blocked_keys[places].astype(jnp.float32)
        picked_values = blocked_values[places].astype(jnp.float32)
        query_part = blocked_queries[index].astype(jnp.float32)
        scores = jnp.einsum("qhgd,lkhd->hgqlk", query_part, picked_keys) * factor
        causal = within[None, None, :] <= within[:, None, None]
        allowed = in_use[None, :, None] & ((listed != seq_id)[None, :, None] | causal)
        scores = jnp.where(allowed, scores, -jnp.inf)
        row_peak = jnp.max(scores, axis=(3, 4))
        weights = jnp.where(allowed, jnp.exp(scores - row_peak[:, :, :, None, None]), 0.0)
        denominator = jnp.sum(weights, axis=(3, 4))
        rounded = lax.optimization_barrier(weights.astype(jnp.bfloat16)).astype(jnp.float32)
        summed = jnp.einsum("hgqlk,lkhd->hgqd", rounded, picked_values)
        normed = summed / denominator[..., None]
        merged_out = jnp.transpose(normed, (2, 0, 1, 3)).reshape(BLOCK_TOKENS, QUERY_HEADS * HEAD_SIZE).astype(jnp.bfloat16)
        norm_part = (row_peak + jnp.log(denominator)).reshape(QUERY_HEADS, BLOCK_TOKENS)
        return merged_out, norm_part

    out_blocks, norm_blocks = lax.map(one_block, block_ids)
    attended = out_blocks.reshape(PROMPT_TOKENS, QUERY_HEADS * HEAD_SIZE)
    log_norm = jnp.transpose(norm_blocks, (1, 0, 2)).reshape(QUERY_HEADS, PROMPT_TOKENS)
    return attended, log_norm
```

```python
import functools
import math

import jax
import jax.numpy as jnp
from jax import lax
from jax.experimental import pallas as pl
from jax.experimental.pallas import tpu as pltpu
from jax.sharding import PartitionSpec as P

HEAD_SIZE = 128
BLOCK_TOKENS = 128
CHUNK = 256
FAR = 1e30
HUGE = 3e38
MESH = pl.DeviceIdType.MESH


def grid_of(count):
    minor = max(d for d in range(1, math.isqrt(count) + 1) if count % d == 0)
    return count // minor, minor


def kernel(
    dims,
    queries,
    keys,
    values,
    block_order,
    live_blocks,
    attended,
    log_norm,
    held,
    raw_queries,
    turned_queries,
    total,
    peak,
    weight_sum,
    leaving,
    limits,
    load_sem,
    send_sem,
    recv_sem,
    swap_send,
    swap_recv,
):
    major, minor, tp_size, kv_local, groups, blocks_here, slots_live = dims
    factor = HEAD_SIZE ** (-0.5)
    scale = factor * math.log2(math.e)
    width = groups * BLOCK_TOKENS
    rows = blocks_here * BLOCK_TOKENS
    me = lax.axis_index("ctx")
    mine = lax.axis_index("tp")
    a, b = me // minor, me % minor

    loads = [
        pltpu.make_async_copy(keys, held.at[me, 0], load_sem.at[0]),
        pltpu.make_async_copy(values, held.at[me, 1], load_sem.at[1]),
        pltpu.make_async_copy(queries, raw_queries, load_sem.at[2]),
    ]
    for load in loads:
        load.start()

    barrier = pltpu.get_barrier_semaphore()
    sides = (
        (a > 0, me - minor),
        (a < major - 1, me + minor),
        (b > 0, me - 1),
        (b < minor - 1, me + 1),
    )
    for there, who in sides:

        @pl.when(there)
        def _(who=who):
            pl.semaphore_signal(barrier, inc=1, device_id={"ctx": who}, device_id_type=MESH)

    for turn in range(1, tp_size):
        peer = (mine + turn) % tp_size
        pl.semaphore_signal(barrier, inc=1, device_id={"tp": peer}, device_id_type=MESH)
    expected = jnp.int32(tp_size - 1)
    for there, _ in sides:
        expected = expected + there.astype(jnp.int32)
    pl.semaphore_wait(barrier, expected)

    def onward(slot, piece, i, j):
        wanted = (
            (j == b) & (i >= a) & (a > 0),
            (j == b) & (i <= a) & (a < major - 1),
            (j >= b) & (b > 0),
            (j <= b) & (b < minor - 1),
        )
        for side in range(4):
            copy = pltpu.make_async_remote_copy(
                src_ref=held.at[slot, piece],
                dst_ref=held.at[slot, piece],
                send_sem=send_sem.at[slot, piece, side],
                recv_sem=recv_sem.at[slot, piece],
                device_id={"ctx": sides[side][1]},
                device_id_type=MESH,
            )
            yield wanted[side], copy

    def send_on(slot, piece, i, j):
        for wanted, copy in onward(slot, piece, i, j):

            @pl.when(wanted)
            def _(copy=copy):
                copy.start()

    def find_limits(slot):
        for query_block in range(blocks_here):
            my_seq = block_order[0, me * blocks_here + query_block]
            found = [jnp.bool_(False)] * blocks_here
            names = [block_order[0, slot * blocks_here + kb] for kb in range(blocks_here)]
            for entry in range(slots_live):
                listed = live_blocks[my_seq, entry]
                found = [f | (listed == name) for f, name in zip(found, names)]
            for kb in range(blocks_here):
                limits[0, query_block * blocks_here + kb] = jnp.where(found[kb], HUGE, -FAR)
                limits[1, query_block * blocks_here + kb] = jnp.where(found[kb], -HUGE, FAR)

    def attend(slot, own):
        find_limits(slot)
        for h in range(kv_local):
            columns = pl.ds(h * HEAD_SIZE, HEAD_SIZE)
            key_part = held[slot, 0, :, columns]
            value_part = jnp.transpose(held[slot, 1, :, columns])

            def one_query_block(query_block, carry):
                caps = [limits[0, query_block * blocks_here + kb] for kb in range(blocks_here)]
                floors = [limits[1, query_block * blocks_here + kb] for kb in range(blocks_here)]
                for start in range(0, width, CHUNK):
                    lanes = pl.ds(start, CHUNK)
                    scores = jnp.dot(
                        key_part,
                        turned_queries[query_block, h, :, lanes],
                        preferred_element_type=jnp.float32,
                    )
                    parts = []
                    for kb in range(blocks_here):
                        part = scores[kb * BLOCK_TOKENS : (kb + 1) * BLOCK_TOKENS]
                        if own:
                            key_at = lax.broadcasted_iota(jnp.int32, part.shape, 0)
                            row_at = lax.broadcasted_iota(jnp.int32, part.shape, 1) % BLOCK_TOKENS
                            reach = jnp.where(query_block == kb, 0, BLOCK_TOKENS)
                            part = jnp.where(key_at <= row_at + reach, part, -FAR)
                        parts.append(part)
                    new_peak = None
                    for part, cap in zip(parts, caps):
                        top = jnp.minimum(jnp.max(part, axis=0, keepdims=True), cap)
                        new_peak = top if new_peak is None else jnp.maximum(new_peak, top)
                    if not own:
                        old_peak = peak[query_block, h, :, lanes]
                        new_peak = jnp.maximum(new_peak, old_peak)
                    peak[query_block, h, :, lanes] = new_peak
                    level = new_peak * scale
                    weights = [
                        jnp.exp2(part * scale - jnp.maximum(level, floor))
                        for part, floor in zip(parts, floors)
                    ]
                    added = None
                    for w in weights:
                        s = jnp.sum(w, axis=0, keepdims=True)
                        added = s if added is None else added + s
                    low = jnp.concatenate([w.astype(jnp.bfloat16) for w in weights], axis=0)
                    product = jnp.dot(value_part, low, preferred_element_type=jnp.float32)
                    if own:
                        weight_sum[query_block, h, :, lanes] = added
                        total[query_block, h, :, lanes] = product
                    else:
                        fade = jnp.exp2((old_peak - new_peak) * scale)
                        weight_sum[query_block, h, :, lanes] = (
                            weight_sum[query_block, h, :, lanes] * fade + added
                        )
                        total[query_block, h, :, lanes] = (
                            total[query_block, h, :, lanes] * fade + product
                        )
                return carry

            lax.fori_loop(0, blocks_here, one_query_block, 0)

    for piece in range(2):
        loads[piece].wait()
        send_on(me, piece, a, b)
    loads[2].wait()

    def turn_block(query_block, carry):
        at = pl.ds(pl.multiple_of(query_block * BLOCK_TOKENS, BLOCK_TOKENS), BLOCK_TOKENS)
        for h in range(kv_local):
            for g in range(groups):
                head = h * groups + g
                turned_queries[query_block, h, :, pl.ds(g * BLOCK_TOKENS, BLOCK_TOKENS)] = (
                    jnp.transpose(raw_queries[at, pl.ds(head * HEAD_SIZE, HEAD_SIZE)])
                )
        return carry

    lax.fori_loop(0, blocks_here, turn_block, 0)
    attend(me, True)

    rounds = (major + minor - 1) * minor * 4

    def place_of(turn):
        far, near = turn // (4 * minor), (turn // 4) % minor
        up, along = (turn // 2) % 2, turn % 2
        reach = far - near
        i = a + reach * (1 - 2 * up)
        j = b + near * (1 - 2 * along)
        fits = (reach >= 0) & (i >= 0) & (i < major) & (j >= 0) & (j < minor)
        fits = fits & ((reach > 0) | (up == 0)) & ((near > 0) | (along == 0))
        return fits, i, j

    def one_shard(turn, carry):
        fits, i, j = place_of(turn)

        @pl.when(fits & (far_from(i, j)))
        def _():
            slot = i * minor + j
            for piece in range(2):
                pltpu.make_async_copy(
                    held.at[slot, piece], held.at[slot, piece], recv_sem.at[slot, piece]
                ).wait()
                send_on(slot, piece, i, j)
            attend(slot, False)

        return carry

    def far_from(i, j):
        return (i != a) | (j != b)

    lax.fori_loop(1, rounds, one_shard, 0)

    per_peer = blocks_here // tp_size
    wide = kv_local * width

    def finish(query_block, h, put):
        at = pl.ds(pl.multiple_of(query_block * BLOCK_TOKENS, BLOCK_TOKENS), BLOCK_TOKENS)
        for g in range(groups):
            lanes = pl.ds(g * BLOCK_TOKENS, BLOCK_TOKENS)
            bottom = weight_sum[query_block, h, :, lanes]
            normed = (total[query_block, h, :, lanes] * (1.0 / bottom)).astype(jnp.bfloat16)
            put(h * groups + g, jnp.transpose(normed))
            log_norm[pl.ds(h * groups + g, 1), at] = (
                peak[query_block, h, :, lanes] * factor + jnp.log(bottom)
            )

    swaps = []
    for turn in range(1, tp_size + 1):
        peer = (mine + turn) % tp_size
        for k in range(per_peer):
            query_block = peer * per_peer + k
            out_rows = pl.ds(k * BLOCK_TOKENS, BLOCK_TOKENS)
            for h in range(kv_local):
                if turn < tp_size:

                    def put(head, tile, query_block=query_block):
                        leaving[query_block, :, pl.ds(head * HEAD_SIZE, HEAD_SIZE)] = tile

                else:

                    def put(head, tile, out_rows=out_rows):
                        at = pl.multiple_of(mine * wide + head * HEAD_SIZE, HEAD_SIZE)
                        attended[out_rows, pl.ds(at, HEAD_SIZE)] = tile

                finish(query_block, h, put)
                if turn < tp_size:
                    source = pl.ds(h * width, width)
                    target = pl.ds(pl.multiple_of(mine * wide + h * width, HEAD_SIZE), width)
                    copy = pltpu.make_async_remote_copy(
                        src_ref=leaving.at[query_block, :, source],
                        dst_ref=attended.at[out_rows, target],
                        send_sem=swap_send.at[turn - 1, k, h],
                        recv_sem=swap_recv.at[turn - 1, k, h],
                        device_id={"tp": peer},
                        device_id_type=MESH,
                    )
                    copy.start()
                    swaps.append(copy)

    def settle(turn, carry):
        fits, i, j = place_of(turn)

        @pl.when(fits)
        def _():
            slot = i * minor + j
            for piece in range(2):
                for wanted, copy in onward(slot, piece, i, j):

                    @pl.when(wanted)
                    def _(copy=copy):
                        copy.wait_send()

        return carry

    lax.fori_loop(0, rounds, settle, 0)
    for copy in swaps:
        copy.wait()


def body(tp_size, ctx_size, queries, rotated_key_rows, ordered_value_rows, block_order, live_blocks):
    tok_rows, own_columns = queries.shape
    kv_columns = rotated_key_rows.shape[1]
    kv_local = kv_columns // HEAD_SIZE
    heads_local = own_columns // HEAD_SIZE
    groups = heads_local // kv_local
    blocks_here = tok_rows // BLOCK_TOKENS
    width = groups * BLOCK_TOKENS
    major, minor = grid_of(ctx_size)
    dims = (major, minor, tp_size, kv_local, groups, blocks_here, live_blocks.shape[1])
    per_peer = blocks_here // tp_size
    whole = pl.BlockSpec(memory_space=pltpu.VMEM)
    small = pl.BlockSpec(memory_space=pltpu.SMEM)
    apart = pl.BlockSpec(memory_space=pl.ANY)
    return pl.pallas_call(
        functools.partial(kernel, dims),
        out_shape=(
            jax.ShapeDtypeStruct((tok_rows // tp_size, own_columns * tp_size), jnp.bfloat16),
            jax.ShapeDtypeStruct((heads_local, tok_rows), jnp.float32),
        ),
        in_specs=[apart, apart, apart, small, small],
        out_specs=(whole, whole),
        scratch_shapes=[
            pltpu.VMEM((ctx_size, 2, tok_rows, kv_columns), jnp.bfloat16),
            pltpu.VMEM((tok_rows, own_columns), jnp.bfloat16),
            pltpu.VMEM((blocks_here, kv_local, HEAD_SIZE, width), jnp.bfloat16),
            pltpu.VMEM((blocks_here, kv_local, HEAD_SIZE, width), jnp.float32),
            pltpu.VMEM((blocks_here, kv_local, 1, width), jnp.float32),
            pltpu.VMEM((blocks_here, kv_local, 1, width), jnp.float32),
            pltpu.VMEM((blocks_here, BLOCK_TOKENS, own_columns), jnp.bfloat16),
            pltpu.SMEM((2, blocks_here * blocks_here), jnp.float32),
            pltpu.SemaphoreType.DMA((3,)),
            pltpu.SemaphoreType.DMA((ctx_size, 2, 4)),
            pltpu.SemaphoreType.DMA((ctx_size, 2)),
            pltpu.SemaphoreType.DMA((tp_size - 1, per_peer, kv_local)),
            pltpu.SemaphoreType.DMA((tp_size - 1, per_peer, kv_local)),
        ],
        compiler_params=pltpu.CompilerParams(collective_id=0, has_side_effects=True),
        name="gather_attend",
    )(queries, rotated_key_rows, ordered_value_rows, block_order.reshape(1, -1), live_blocks)


def solution(mesh):
    placed = (
        P(("rep", "ctx"), "tp"),
        P(("rep", "ctx"), "tp"),
        P(("rep", "ctx"), "tp"),
        P("rep"),
        P("rep", None),
    )
    return jax.shard_map(
        functools.partial(body, mesh.shape["tp"], mesh.shape["ctx"]),
        mesh=mesh,
        in_specs=placed,
        out_specs=(P(("rep", "ctx", "tp"), None), P(("rep", "tp"), "ctx")),
        check_vma=False,
    )
```

```python
import functools
import math

import jax
import jax.numpy as jnp
from jax import lax
from jax.experimental import pallas as pl
from jax.experimental.pallas import tpu as pltpu
from jax.sharding import PartitionSpec as P

HEAD_SIZE = 128
BLOCK_TOKENS = 128
CHUNK = 256
STRIP = 16
SLOTS = 3
FAR = 1e30
HUGE = 3e38
MESH = pl.DeviceIdType.MESH


def grid_of(count):
    minor = max(d for d in range(1, math.isqrt(count) + 1) if count % d == 0)
    return count // minor, minor


def kernel(
    dims,
    queries,
    keys,
    values,
    block_order,
    live_blocks,
    attended,
    log_norm,
    held,
    raw_queries,
    turned_queries,
    total,
    peak,
    weight_sum,
    leaving,
    limits,
    scores,
    load_sem,
    send_sem,
    recv_sem,
    swap_send,
    swap_recv,
):
    major, minor, tp_size, kv_local, groups, blocks_here, slots_live = dims
    factor = HEAD_SIZE ** (-0.5)
    scale = factor * math.log2(math.e)
    width = groups * BLOCK_TOKENS
    rows = blocks_here * BLOCK_TOKENS
    me = lax.axis_index("ctx")
    mine = lax.axis_index("tp")
    a, b = me // minor, me % minor

    loads = [
        pltpu.make_async_copy(keys, held.at[me, 0], load_sem.at[0]),
        pltpu.make_async_copy(values, held.at[me, 1], load_sem.at[1]),
        pltpu.make_async_copy(queries, raw_queries, load_sem.at[2]),
    ]
    for load in loads:
        load.start()

    barrier = pltpu.get_barrier_semaphore()
    sides = (
        (a > 0, me - minor),
        (a < major - 1, me + minor),
        (b > 0, me - 1),
        (b < minor - 1, me + 1),
    )
    for there, who in sides:

        @pl.when(there)
        def _(who=who):
            pl.semaphore_signal(barrier, inc=1, device_id={"ctx": who}, device_id_type=MESH)

    for turn in range(1, tp_size):
        peer = (mine + turn) % tp_size
        pl.semaphore_signal(barrier, inc=1, device_id={"tp": peer}, device_id_type=MESH)
    expected = jnp.int32(tp_size - 1)
    for there, _ in sides:
        expected = expected + there.astype(jnp.int32)
    pl.semaphore_wait(barrier, expected)

    def onward(slot, piece, i, j):
        wanted = (
            (j == b) & (i >= a) & (a > 0),
            (j == b) & (i <= a) & (a < major - 1),
            (j >= b) & (b > 0),
            (j <= b) & (b < minor - 1),
        )
        for side in range(4):
            copy = pltpu.make_async_remote_copy(
                src_ref=held.at[slot, piece],
                dst_ref=held.at[slot, piece],
                send_sem=send_sem.at[slot, piece, side],
                recv_sem=recv_sem.at[slot, piece],
                device_id={"ctx": sides[side][1]},
                device_id_type=MESH,
            )
            yield wanted[side], copy

    def send_on(slot, piece, i, j):
        for wanted, copy in onward(slot, piece, i, j):

            @pl.when(wanted)
            def _(copy=copy):
                copy.start()

    def find_limits(slot):
        for query_block in range(blocks_here):
            my_seq = block_order[0, me * blocks_here + query_block]
            found = [jnp.bool_(False)] * blocks_here
            names = [block_order[0, slot * blocks_here + kb] for kb in range(blocks_here)]
            for entry in range(slots_live):
                listed = live_blocks[my_seq, entry]
                found = [f | (listed == name) for f, name in zip(found, names)]
            for kb in range(blocks_here):
                limits[0, query_block * blocks_here + kb] = jnp.where(found[kb], HUGE, -FAR)
                limits[1, query_block * blocks_here + kb] = jnp.where(found[kb], -HUGE, FAR)

    def attend(slot, own):
        find_limits(slot)
        keys_here = blocks_here * BLOCK_TOKENS
        units = [
            (query_block, h, start)
            for h in range(kv_local)
            for query_block in range(blocks_here)
            for start in range(0, width, CHUNK)
        ]
        turned_values = [
            jnp.transpose(held[slot, 1, :, pl.ds(h * HEAD_SIZE, HEAD_SIZE)])
            for h in range(kv_local)
        ]

        def score(u):
            query_block, h, start = units[u]
            part = jnp.dot(
                held[slot, 0, :, pl.ds(h * HEAD_SIZE, HEAD_SIZE)],
                turned_queries[query_block, h, :, pl.ds(start, CHUNK)],
                preferred_element_type=jnp.float32,
            )
            tops = []
            for kb in range(blocks_here):
                block = part[kb * BLOCK_TOKENS : (kb + 1) * BLOCK_TOKENS]
                if own and kb == query_block:
                    key_at = lax.broadcasted_iota(jnp.int32, block.shape, 0)
                    row_at = lax.broadcasted_iota(jnp.int32, block.shape, 1) % BLOCK_TOKENS
                    block = jnp.where(key_at <= row_at, block, -FAR)
                scores[u % SLOTS, pl.ds(kb * BLOCK_TOKENS, BLOCK_TOKENS), :] = block
                tops.append(jnp.max(block, axis=0, keepdims=True))
            return tops

        def absorb(u, tops):
            query_block, h, start = units[u]
            lanes = pl.ds(start, CHUNK)
            first = query_block * blocks_here
            new_peak = None
            for kb, top in enumerate(tops):
                top = jnp.minimum(top, limits[0, first + kb])
                new_peak = top if new_peak is None else jnp.maximum(new_peak, top)
            if not own:
                old_peak = peak[query_block, h, :, lanes]
                new_peak = jnp.maximum(new_peak, old_peak)
            peak[query_block, h, :, lanes] = new_peak
            level = new_peak * scale
            added = None
            low = []
            for kb in range(blocks_here):
                floor = jnp.maximum(level, limits[1, first + kb])
                for at in range(kb * BLOCK_TOKENS, (kb + 1) * BLOCK_TOKENS, STRIP):
                    w = jnp.exp2(scores[u % SLOTS, pl.ds(at, STRIP), :] * scale - floor)
                    added = w if added is None else added + w
                    low.append(w.astype(jnp.bfloat16))
            added = jnp.sum(added, axis=0, keepdims=True)
            product = jnp.dot(
                turned_values[h],
                jnp.concatenate(low, axis=0),
                preferred_element_type=jnp.float32,
            )
            if own:
                weight_sum[query_block, h, :, lanes] = added
                total[query_block, h, :, lanes] = product
            else:
                fade = jnp.exp2((old_peak - new_peak) * scale)
                weight_sum[query_block, h, :, lanes] = (
                    weight_sum[query_block, h, :, lanes] * fade + added
                )
                total[query_block, h, :, lanes] = total[query_block, h, :, lanes] * fade + product

        waiting = [score(u) for u in range(SLOTS - 1)]
        for u in range(len(units)):
            if u + SLOTS - 1 < len(units):
                waiting.append(score(u + SLOTS - 1))
            absorb(u, waiting[u])

    for piece in range(2):
        loads[piece].wait()
        send_on(me, piece, a, b)
    loads[2].wait()

    def turn_block(query_block, carry):
        at = pl.ds(pl.multiple_of(query_block * BLOCK_TOKENS, BLOCK_TOKENS), BLOCK_TOKENS)
        for h in range(kv_local):
            for g in range(groups):
                head = h * groups + g
                turned_queries[query_block, h, :, pl.ds(g * BLOCK_TOKENS, BLOCK_TOKENS)] = (
                    jnp.transpose(raw_queries[at, pl.ds(head * HEAD_SIZE, HEAD_SIZE)])
                )
        return carry

    lax.fori_loop(0, blocks_here, turn_block, 0)
    attend(me, True)

    rounds = (major + minor - 1) * minor * 4

    def place_of(turn):
        far, near = turn // (4 * minor), (turn // 4) % minor
        up, along = (turn // 2) % 2, turn % 2
        reach = far - near
        i = a + reach * (1 - 2 * up)
        j = b + near * (1 - 2 * along)
        fits = (reach >= 0) & (i >= 0) & (i < major) & (j >= 0) & (j < minor)
        fits = fits & ((reach > 0) | (up == 0)) & ((near > 0) | (along == 0))
        return fits, i, j

    def one_shard(turn, carry):
        fits, i, j = place_of(turn)

        @pl.when(fits & (far_from(i, j)))
        def _():
            slot = i * minor + j
            for piece in range(2):
                pltpu.make_async_copy(
                    held.at[slot, piece], held.at[slot, piece], recv_sem.at[slot, piece]
                ).wait()
                send_on(slot, piece, i, j)
            attend(slot, False)

        return carry

    def far_from(i, j):
        return (i != a) | (j != b)

    lax.fori_loop(1, rounds, one_shard, 0)

    per_peer = blocks_here // tp_size
    wide = kv_local * width

    def finish(query_block, h, put):
        at = pl.ds(pl.multiple_of(query_block * BLOCK_TOKENS, BLOCK_TOKENS), BLOCK_TOKENS)
        for g in range(groups):
            lanes = pl.ds(g * BLOCK_TOKENS, BLOCK_TOKENS)
            bottom = weight_sum[query_block, h, :, lanes]
            normed = (total[query_block, h, :, lanes] * (1.0 / bottom)).astype(jnp.bfloat16)
            put(h * groups + g, jnp.transpose(normed))
            log_norm[pl.ds(h * groups + g, 1), at] = (
                peak[query_block, h, :, lanes] * factor + jnp.log(bottom)
            )

    swaps = []
    for turn in range(1, tp_size + 1):
        peer = (mine + turn) % tp_size
        for k in range(per_peer):
            query_block = peer * per_peer + k
            out_rows = pl.ds(k * BLOCK_TOKENS, BLOCK_TOKENS)
            for h in range(kv_local):
                if turn < tp_size:

                    def put(head, tile, query_block=query_block):
                        leaving[query_block, :, pl.ds(head * HEAD_SIZE, HEAD_SIZE)] = tile

                else:

                    def put(head, tile, out_rows=out_rows):
                        at = pl.multiple_of(mine * wide + head * HEAD_SIZE, HEAD_SIZE)
                        attended[out_rows, pl.ds(at, HEAD_SIZE)] = tile

                finish(query_block, h, put)
                if turn < tp_size:
                    source = pl.ds(h * width, width)
                    target = pl.ds(pl.multiple_of(mine * wide + h * width, HEAD_SIZE), width)
                    copy = pltpu.make_async_remote_copy(
                        src_ref=leaving.at[query_block, :, source],
                        dst_ref=attended.at[out_rows, target],
                        send_sem=swap_send.at[turn - 1, k, h],
                        recv_sem=swap_recv.at[turn - 1, k, h],
                        device_id={"tp": peer},
                        device_id_type=MESH,
                    )
                    copy.start()
                    swaps.append(copy)

    def settle(turn, carry):
        fits, i, j = place_of(turn)

        @pl.when(fits)
        def _():
            slot = i * minor + j
            for piece in range(2):
                for wanted, copy in onward(slot, piece, i, j):

                    @pl.when(wanted)
                    def _(copy=copy):
                        copy.wait_send()

        return carry

    lax.fori_loop(0, rounds, settle, 0)
    for copy in swaps:
        copy.wait()


def body(tp_size, ctx_size, queries, rotated_key_rows, ordered_value_rows, block_order, live_blocks):
    tok_rows, own_columns = queries.shape
    kv_columns = rotated_key_rows.shape[1]
    kv_local = kv_columns // HEAD_SIZE
    heads_local = own_columns // HEAD_SIZE
    groups = heads_local // kv_local
    blocks_here = tok_rows // BLOCK_TOKENS
    width = groups * BLOCK_TOKENS
    major, minor = grid_of(ctx_size)
    dims = (major, minor, tp_size, kv_local, groups, blocks_here, live_blocks.shape[1])
    per_peer = blocks_here // tp_size
    whole = pl.BlockSpec(memory_space=pltpu.VMEM)
    small = pl.BlockSpec(memory_space=pltpu.SMEM)
    apart = pl.BlockSpec(memory_space=pl.ANY)
    return pl.pallas_call(
        functools.partial(kernel, dims),
        out_shape=(
            jax.ShapeDtypeStruct((tok_rows // tp_size, own_columns * tp_size), jnp.bfloat16),
            jax.ShapeDtypeStruct((heads_local, tok_rows), jnp.float32),
        ),
        in_specs=[apart, apart, apart, small, small],
        out_specs=(whole, whole),
        scratch_shapes=[
            pltpu.VMEM((ctx_size, 2, tok_rows, kv_columns), jnp.bfloat16),
            pltpu.VMEM((tok_rows, own_columns), jnp.bfloat16),
            pltpu.VMEM((blocks_here, kv_local, HEAD_SIZE, width), jnp.bfloat16),
            pltpu.VMEM((blocks_here, kv_local, HEAD_SIZE, width), jnp.float32),
            pltpu.VMEM((blocks_here, kv_local, 1, width), jnp.float32),
            pltpu.VMEM((blocks_here, kv_local, 1, width), jnp.float32),
            pltpu.VMEM((blocks_here, BLOCK_TOKENS, own_columns), jnp.bfloat16),
            pltpu.SMEM((2, blocks_here * blocks_here), jnp.float32),
            pltpu.VMEM((SLOTS, tok_rows, CHUNK), jnp.float32),
            pltpu.SemaphoreType.DMA((3,)),
            pltpu.SemaphoreType.DMA((ctx_size, 2, 4)),
            pltpu.SemaphoreType.DMA((ctx_size, 2)),
            pltpu.SemaphoreType.DMA((tp_size - 1, per_peer, kv_local)),
            pltpu.SemaphoreType.DMA((tp_size - 1, per_peer, kv_local)),
        ],
        compiler_params=pltpu.CompilerParams(collective_id=0, has_side_effects=True),
        name="gather_attend",
    )(queries, rotated_key_rows, ordered_value_rows, block_order.reshape(1, -1), live_blocks)


def solution(mesh):
    placed = (
        P(("rep", "ctx"), "tp"),
        P(("rep", "ctx"), "tp"),
        P(("rep", "ctx"), "tp"),
        P("rep"),
        P("rep", None),
    )
    return jax.shard_map(
        functools.partial(body, mesh.shape["tp"], mesh.shape["ctx"]),
        mesh=mesh,
        in_specs=placed,
        out_specs=(P(("rep", "ctx", "tp"), None), P(("rep", "tp"), "ctx")),
        check_vma=False,
    )
```

```python
import functools
import math

import jax
import jax.numpy as jnp
from jax import lax
from jax.experimental import pallas as pl
from jax.experimental.pallas import tpu as pltpu
from jax.sharding import PartitionSpec as P

HEAD_SIZE = 128
BLOCK_TOKENS = 128
CHUNK = 256
STRIP = 16
SLOTS = 3
FAR = 1e30
HUGE = 3e38
MESH = pl.DeviceIdType.MESH


def grid_of(count):
    minor = max(d for d in range(1, math.isqrt(count) + 1) if count % d == 0)
    return count // minor, minor


def kernel(
    dims,
    queries,
    keys,
    values,
    block_order,
    live_blocks,
    attended,
    log_norm,
    held,
    raw_queries,
    turned_queries,
    total,
    peak,
    weight_sum,
    leaving,
    limits,
    scores,
    load_sem,
    send_sem,
    recv_sem,
    swap_send,
    swap_recv,
):
    major, minor, tp_size, kv_local, groups, blocks_here, slots_live = dims
    factor = HEAD_SIZE ** (-0.5)
    scale = factor * math.log2(math.e)
    width = groups * BLOCK_TOKENS
    rows = blocks_here * BLOCK_TOKENS
    me = lax.axis_index("ctx")
    mine = lax.axis_index("tp")
    a, b = me // minor, me % minor

    loads = [
        pltpu.make_async_copy(keys, held.at[me, 0], load_sem.at[0]),
        pltpu.make_async_copy(values, held.at[me, 1], load_sem.at[1]),
        pltpu.make_async_copy(queries, raw_queries, load_sem.at[2]),
    ]
    for load in loads:
        load.start()

    barrier = pltpu.get_barrier_semaphore()
    sides = (
        (a > 0, me - minor),
        (a < major - 1, me + minor),
        (b > 0, me - 1),
        (b < minor - 1, me + 1),
    )
    for there, who in sides:

        @pl.when(there)
        def _(who=who):
            pl.semaphore_signal(barrier, inc=1, device_id={"ctx": who}, device_id_type=MESH)

    for turn in range(1, tp_size):
        peer = (mine + turn) % tp_size
        pl.semaphore_signal(barrier, inc=1, device_id={"tp": peer}, device_id_type=MESH)
    expected = jnp.int32(tp_size - 1)
    for there, _ in sides:
        expected = expected + there.astype(jnp.int32)
    pl.semaphore_wait(barrier, expected)

    def onward(slot, piece, i, j):
        wanted = (
            (j == b) & (i >= a) & (a > 0),
            (j == b) & (i <= a) & (a < major - 1),
            (j >= b) & (b > 0),
            (j <= b) & (b < minor - 1),
        )
        for side in range(4):
            copy = pltpu.make_async_remote_copy(
                src_ref=held.at[slot, piece],
                dst_ref=held.at[slot, piece],
                send_sem=send_sem.at[slot, piece, side],
                recv_sem=recv_sem.at[slot, piece],
                device_id={"ctx": sides[side][1]},
                device_id_type=MESH,
            )
            yield wanted[side], copy

    def send_on(slot, piece, i, j):
        for wanted, copy in onward(slot, piece, i, j):

            @pl.when(wanted)
            def _(copy=copy):
                copy.start()

    def find_limits(slot):
        for query_block in range(blocks_here):
            my_seq = block_order[0, me * blocks_here + query_block]
            found = [jnp.bool_(False)] * blocks_here
            names = [block_order[0, slot * blocks_here + kb] for kb in range(blocks_here)]
            for entry in range(slots_live):
                listed = live_blocks[my_seq, entry]
                found = [f | (listed == name) for f, name in zip(found, names)]
            for kb in range(blocks_here):
                limits[0, query_block * blocks_here + kb] = jnp.where(found[kb], HUGE, -FAR)
                limits[1, query_block * blocks_here + kb] = jnp.where(found[kb], -HUGE, FAR)

    def attend(slot, own):
        find_limits(slot)
        keys_here = blocks_here * BLOCK_TOKENS
        units = [
            (query_block, h, start)
            for h in range(kv_local)
            for query_block in range(blocks_here)
            for start in range(0, width, CHUNK)
        ]
        turned_values = [
            jnp.transpose(held[slot, 1, :, pl.ds(h * HEAD_SIZE, HEAD_SIZE)])
            for h in range(kv_local)
        ]

        def score(u):
            query_block, h, start = units[u]
            part = jnp.dot(
                held[slot, 0, :, pl.ds(h * HEAD_SIZE, HEAD_SIZE)],
                turned_queries[query_block, h, :, pl.ds(start, CHUNK)],
                preferred_element_type=jnp.float32,
            )
            tops = []
            for kb in range(blocks_here):
                block = part[kb * BLOCK_TOKENS : (kb + 1) * BLOCK_TOKENS]
                if own and kb == query_block:
                    key_at = lax.broadcasted_iota(jnp.int32, block.shape, 0)
                    row_at = lax.broadcasted_iota(jnp.int32, block.shape, 1) % BLOCK_TOKENS
                    block = jnp.where(key_at <= row_at, block, -FAR)
                scores[u % SLOTS, pl.ds(kb * BLOCK_TOKENS, BLOCK_TOKENS), :] = block
                tops.append(jnp.max(block, axis=0, keepdims=True))
            return tops

        def absorb(u, tops):
            query_block, h, start = units[u]
            lanes = pl.ds(start, CHUNK)
            first = query_block * blocks_here
            new_peak = None
            for kb, top in enumerate(tops):
                top = jnp.minimum(top, limits[0, first + kb])
                new_peak = top if new_peak is None else jnp.maximum(new_peak, top)
            if not own:
                old_peak = peak[query_block, h, :, lanes]
                new_peak = jnp.maximum(new_peak, old_peak)
            peak[query_block, h, :, lanes] = new_peak
            level = new_peak * scale
            added = None
            low = []
            for kb in range(blocks_here):
                floor = jnp.maximum(level, limits[1, first + kb])
                for at in range(kb * BLOCK_TOKENS, (kb + 1) * BLOCK_TOKENS, STRIP):
                    w = jnp.exp2(scores[u % SLOTS, pl.ds(at, STRIP), :] * scale - floor)
                    added = w if added is None else added + w
                    low.append(w.astype(jnp.bfloat16))
            added = jnp.sum(added, axis=0, keepdims=True)
            product = jnp.dot(
                turned_values[h],
                jnp.concatenate(low, axis=0),
                preferred_element_type=jnp.float32,
            )
            if own:
                weight_sum[query_block, h, :, lanes] = added
                total[query_block, h, :, lanes] = product
            else:
                fade = jnp.exp2((old_peak - new_peak) * scale)
                weight_sum[query_block, h, :, lanes] = (
                    weight_sum[query_block, h, :, lanes] * fade + added
                )
                total[query_block, h, :, lanes] = total[query_block, h, :, lanes] * fade + product

        waiting = [score(u) for u in range(SLOTS - 1)]
        for u in range(len(units)):
            if u + SLOTS - 1 < len(units):
                waiting.append(score(u + SLOTS - 1))
            absorb(u, waiting[u])

    for piece in range(2):
        loads[piece].wait()
        send_on(me, piece, a, b)
    loads[2].wait()

    def turn_block(query_block, carry):
        at = pl.ds(pl.multiple_of(query_block * BLOCK_TOKENS, BLOCK_TOKENS), BLOCK_TOKENS)
        for h in range(kv_local):
            for g in range(groups):
                head = h * groups + g
                turned_queries[query_block, h, :, pl.ds(g * BLOCK_TOKENS, BLOCK_TOKENS)] = (
                    jnp.transpose(raw_queries[at, pl.ds(head * HEAD_SIZE, HEAD_SIZE)])
                )
        return carry

    lax.fori_loop(0, blocks_here, turn_block, 0)
    attend(me, True)

    rounds = (major + minor - 1) * minor * 4

    def place_of(turn):
        far, near = turn // (4 * minor), (turn // 4) % minor
        up, along = (turn // 2) % 2, turn % 2
        reach = far - near
        i = a + reach * (1 - 2 * up)
        j = b + near * (1 - 2 * along)
        fits = (reach >= 0) & (i >= 0) & (i < major) & (j >= 0) & (j < minor)
        fits = fits & ((reach > 0) | (up == 0)) & ((near > 0) | (along == 0))
        return fits, i, j

    def one_shard(turn, carry):
        fits, i, j = place_of(turn)

        @pl.when(fits & (far_from(i, j)))
        def _():
            slot = i * minor + j
            for piece in range(2):
                pltpu.make_async_copy(
                    held.at[slot, piece], held.at[slot, piece], recv_sem.at[slot, piece]
                ).wait()
                send_on(slot, piece, i, j)
            attend(slot, False)

        return carry

    def far_from(i, j):
        return (i != a) | (j != b)

    lax.fori_loop(1, rounds, one_shard, 0)

    per_peer = blocks_here // tp_size
    wide = kv_local * width

    def finish(query_block, h, put):
        at = pl.ds(pl.multiple_of(query_block * BLOCK_TOKENS, BLOCK_TOKENS), BLOCK_TOKENS)
        for g in range(groups):
            lanes = pl.ds(g * BLOCK_TOKENS, BLOCK_TOKENS)
            bottom = weight_sum[query_block, h, :, lanes]
            normed = (total[query_block, h, :, lanes] * (1.0 / bottom)).astype(jnp.bfloat16)
            put(h * groups + g, jnp.transpose(normed))
            log_norm[pl.ds(h * groups + g, 1), at] = (
                peak[query_block, h, :, lanes] * factor + jnp.log(bottom)
            )

    swaps = []
    for turn in range(1, tp_size + 1):
        peer = (mine + turn) % tp_size
        for k in range(per_peer):
            query_block = peer * per_peer + k
            out_rows = pl.ds(k * BLOCK_TOKENS, BLOCK_TOKENS)
            for h in range(kv_local):
                if turn < tp_size:

                    def put(head, tile, query_block=query_block):
                        leaving[query_block, :, pl.ds(head * HEAD_SIZE, HEAD_SIZE)] = tile

                else:

                    def put(head, tile, out_rows=out_rows):
                        at = pl.multiple_of(mine * wide + head * HEAD_SIZE, HEAD_SIZE)
                        attended[out_rows, pl.ds(at, HEAD_SIZE)] = tile

                finish(query_block, h, put)
                if turn < tp_size:
                    source = pl.ds(h * width, width)
                    target = pl.ds(pl.multiple_of(mine * wide + h * width, HEAD_SIZE), width)
                    copy = pltpu.make_async_remote_copy(
                        src_ref=leaving.at[query_block, :, source],
                        dst_ref=attended.at[out_rows, target],
                        send_sem=swap_send.at[turn - 1, k, h],
                        recv_sem=swap_recv.at[turn - 1, k, h],
                        device_id={"tp": peer},
                        device_id_type=MESH,
                    )
                    copy.start()
                    swaps.append(copy)

    def settle(turn, carry):
        fits, i, j = place_of(turn)

        @pl.when(fits)
        def _():
            slot = i * minor + j
            for piece in range(2):
                for wanted, copy in onward(slot, piece, i, j):

                    @pl.when(wanted)
                    def _(copy=copy):
                        copy.wait_send()

        return carry

    lax.fori_loop(0, rounds, settle, 0)
    for copy in swaps:
        copy.wait()


def body(tp_size, ctx_size, queries, rotated_key_rows, ordered_value_rows, block_order, live_blocks):
    tok_rows, own_columns = queries.shape
    kv_columns = rotated_key_rows.shape[1]
    kv_local = kv_columns // HEAD_SIZE
    heads_local = own_columns // HEAD_SIZE
    groups = heads_local // kv_local
    blocks_here = tok_rows // BLOCK_TOKENS
    width = groups * BLOCK_TOKENS
    major, minor = grid_of(ctx_size)
    dims = (major, minor, tp_size, kv_local, groups, blocks_here, live_blocks.shape[1])
    per_peer = blocks_here // tp_size
    whole = pl.BlockSpec(memory_space=pltpu.VMEM)
    small = pl.BlockSpec(memory_space=pltpu.SMEM)
    apart = pl.BlockSpec(memory_space=pl.ANY)
    results = pl.pallas_call(
        functools.partial(kernel, dims),
        out_shape=(
            pltpu.VMEM((tok_rows // tp_size, own_columns * tp_size), jnp.bfloat16),
            pltpu.VMEM((heads_local, tok_rows), jnp.float32),
        ),
        in_specs=[apart, apart, apart, small, small],
        out_specs=(whole, whole),
        scratch_shapes=[
            pltpu.VMEM((ctx_size, 2, tok_rows, kv_columns), jnp.bfloat16),
            pltpu.VMEM((tok_rows, own_columns), jnp.bfloat16),
            pltpu.VMEM((blocks_here, kv_local, HEAD_SIZE, width), jnp.bfloat16),
            pltpu.VMEM((blocks_here, kv_local, HEAD_SIZE, width), jnp.float32),
            pltpu.VMEM((blocks_here, kv_local, 1, width), jnp.float32),
            pltpu.VMEM((blocks_here, kv_local, 1, width), jnp.float32),
            pltpu.VMEM((blocks_here, BLOCK_TOKENS, own_columns), jnp.bfloat16),
            pltpu.SMEM((2, blocks_here * blocks_here), jnp.float32),
            pltpu.VMEM((SLOTS, tok_rows, CHUNK), jnp.float32),
            pltpu.SemaphoreType.DMA((3,)),
            pltpu.SemaphoreType.DMA((ctx_size, 2, 4)),
            pltpu.SemaphoreType.DMA((ctx_size, 2)),
            pltpu.SemaphoreType.DMA((tp_size - 1, per_peer, kv_local)),
            pltpu.SemaphoreType.DMA((tp_size - 1, per_peer, kv_local)),
        ],
        compiler_params=pltpu.CompilerParams(collective_id=0, has_side_effects=True),
        name="gather_attend",
    )(queries, rotated_key_rows, ordered_value_rows, block_order.reshape(1, -1), live_blocks)
    return results


def solution(mesh):
    placed = (
        P(("rep", "ctx"), "tp"),
        P(("rep", "ctx"), "tp"),
        P(("rep", "ctx"), "tp"),
        P("rep"),
        P("rep", None),
    )
    return jax.shard_map(
        functools.partial(body, mesh.shape["tp"], mesh.shape["ctx"]),
        mesh=mesh,
        in_specs=placed,
        out_specs=(P(("rep", "ctx", "tp"), None), P(("rep", "tp"), "ctx")),
        check_vma=False,
    )
```

```python
import functools
import math

import jax
import jax.numpy as jnp
from jax import lax
from jax.experimental import pallas as pl
from jax.experimental.pallas import tpu as pltpu
from jax.sharding import PartitionSpec as P

HEAD_SIZE = 128
BLOCK_TOKENS = 128
CHUNK = 256
STRIP = 16
SLOTS = 4
FAR = 1e30
HUGE = 3e38
MESH = pl.DeviceIdType.MESH


def grid_of(count):
    minor = max(d for d in range(1, math.isqrt(count) + 1) if count % d == 0)
    return count // minor, minor


def kernel(
    dims,
    queries,
    keys,
    values,
    block_order,
    live_blocks,
    attended,
    log_norm,
    held,
    raw_queries,
    turned_queries,
    total,
    peak,
    weight_sum,
    leaving,
    limits,
    scores,
    load_sem,
    send_sem,
    recv_sem,
    swap_send,
    swap_recv,
):
    major, minor, tp_size, kv_local, groups, blocks_here, slots_live = dims
    factor = HEAD_SIZE ** (-0.5)
    scale = factor * math.log2(math.e)
    width = groups * BLOCK_TOKENS
    rows = blocks_here * BLOCK_TOKENS
    me = lax.axis_index("ctx")
    mine = lax.axis_index("tp")
    a, b = me // minor, me % minor

    loads = [
        pltpu.make_async_copy(keys, held.at[me, 0], load_sem.at[0]),
        pltpu.make_async_copy(values, held.at[me, 1], load_sem.at[1]),
        pltpu.make_async_copy(queries, raw_queries, load_sem.at[2]),
    ]
    for load in loads:
        load.start()

    barrier = pltpu.get_barrier_semaphore()
    sides = (
        (a > 0, me - minor),
        (a < major - 1, me + minor),
        (b > 0, me - 1),
        (b < minor - 1, me + 1),
    )
    for there, who in sides:

        @pl.when(there)
        def _(who=who):
            pl.semaphore_signal(barrier, inc=1, device_id={"ctx": who}, device_id_type=MESH)

    for turn in range(1, tp_size):
        peer = (mine + turn) % tp_size
        pl.semaphore_signal(barrier, inc=1, device_id={"tp": peer}, device_id_type=MESH)
    expected = jnp.int32(tp_size - 1)
    for there, _ in sides:
        expected = expected + there.astype(jnp.int32)
    pl.semaphore_wait(barrier, expected)

    def onward(slot, piece, i, j):
        wanted = (
            (j == b) & (i >= a) & (a > 0),
            (j == b) & (i <= a) & (a < major - 1),
            (j >= b) & (b > 0),
            (j <= b) & (b < minor - 1),
        )
        for side in range(4):
            copy = pltpu.make_async_remote_copy(
                src_ref=held.at[slot, piece],
                dst_ref=held.at[slot, piece],
                send_sem=send_sem.at[slot, piece, side],
                recv_sem=recv_sem.at[slot, piece],
                device_id={"ctx": sides[side][1]},
                device_id_type=MESH,
            )
            yield wanted[side], copy

    def send_on(slot, piece, i, j):
        for wanted, copy in onward(slot, piece, i, j):

            @pl.when(wanted)
            def _(copy=copy):
                copy.start()

    def find_limits(slot):
        for query_block in range(blocks_here):
            my_seq = block_order[0, me * blocks_here + query_block]
            found = [jnp.bool_(False)] * blocks_here
            names = [block_order[0, slot * blocks_here + kb] for kb in range(blocks_here)]
            for entry in range(slots_live):
                listed = live_blocks[my_seq, entry]
                found = [f | (listed == name) for f, name in zip(found, names)]
            for kb in range(blocks_here):
                limits[0, query_block * blocks_here + kb] = jnp.where(found[kb], HUGE, -FAR)
                limits[1, query_block * blocks_here + kb] = jnp.where(found[kb], -HUGE, FAR)

    def attend(slot, own):
        find_limits(slot)
        keys_here = blocks_here * BLOCK_TOKENS
        units = [
            (query_block, h, start)
            for h in range(kv_local)
            for query_block in range(blocks_here)
            for start in range(0, width, CHUNK)
        ]
        turned_values = [
            jnp.transpose(held[slot, 1, :, pl.ds(h * HEAD_SIZE, HEAD_SIZE)])
            for h in range(kv_local)
        ]

        def score(u):
            query_block, h, start = units[u]
            part = jnp.dot(
                held[slot, 0, :, pl.ds(h * HEAD_SIZE, HEAD_SIZE)],
                turned_queries[query_block, h, :, pl.ds(start, CHUNK)],
                preferred_element_type=jnp.float32,
            )
            tops = []
            for kb in range(blocks_here):
                block = part[kb * BLOCK_TOKENS : (kb + 1) * BLOCK_TOKENS]
                if own and kb == query_block:
                    key_at = lax.broadcasted_iota(jnp.int32, block.shape, 0)
                    row_at = lax.broadcasted_iota(jnp.int32, block.shape, 1) % BLOCK_TOKENS
                    block = jnp.where(key_at <= row_at, block, -FAR)
                scores[u % SLOTS, pl.ds(kb * BLOCK_TOKENS, BLOCK_TOKENS), :] = block
                tops.append(jnp.max(block, axis=0, keepdims=True))
            return tops

        def absorb(u, tops):
            query_block, h, start = units[u]
            lanes = pl.ds(start, CHUNK)
            first = query_block * blocks_here
            new_peak = None
            for kb, top in enumerate(tops):
                top = jnp.minimum(top, limits[0, first + kb])
                new_peak = top if new_peak is None else jnp.maximum(new_peak, top)
            if not own:
                old_peak = peak[query_block, h, :, lanes]
                new_peak = jnp.maximum(new_peak, old_peak)
            peak[query_block, h, :, lanes] = new_peak
            level = new_peak * scale
            added = None
            low = []
            for kb in range(blocks_here):
                floor = jnp.maximum(level, limits[1, first + kb])
                for at in range(kb * BLOCK_TOKENS, (kb + 1) * BLOCK_TOKENS, STRIP):
                    w = jnp.exp2(scores[u % SLOTS, pl.ds(at, STRIP), :] * scale - floor)
                    added = w if added is None else added + w
                    low.append(w.astype(jnp.bfloat16))
            added = jnp.sum(added, axis=0, keepdims=True)
            product = jnp.dot(
                turned_values[h],
                jnp.concatenate(low, axis=0),
                preferred_element_type=jnp.float32,
            )
            if own:
                weight_sum[query_block, h, :, lanes] = added
                total[query_block, h, :, lanes] = product
            else:
                fade = jnp.exp2((old_peak - new_peak) * scale)
                weight_sum[query_block, h, :, lanes] = (
                    weight_sum[query_block, h, :, lanes] * fade + added
                )
                total[query_block, h, :, lanes] = total[query_block, h, :, lanes] * fade + product

        waiting = [score(u) for u in range(SLOTS - 1)]
        for u in range(len(units)):
            if u + SLOTS - 1 < len(units):
                waiting.append(score(u + SLOTS - 1))
            absorb(u, waiting[u])

    for piece in range(2):
        loads[piece].wait()
        send_on(me, piece, a, b)
    loads[2].wait()

    def turn_block(query_block, carry):
        at = pl.ds(pl.multiple_of(query_block * BLOCK_TOKENS, BLOCK_TOKENS), BLOCK_TOKENS)
        for h in range(kv_local):
            for g in range(groups):
                head = h * groups + g
                turned_queries[query_block, h, :, pl.ds(g * BLOCK_TOKENS, BLOCK_TOKENS)] = (
                    jnp.transpose(raw_queries[at, pl.ds(head * HEAD_SIZE, HEAD_SIZE)])
                )
        return carry

    lax.fori_loop(0, blocks_here, turn_block, 0)
    attend(me, True)

    rounds = (major + minor - 1) * minor * 4

    def place_of(turn):
        far, near = turn // (4 * minor), (turn // 4) % minor
        up, along = (turn // 2) % 2, turn % 2
        reach = far - near
        i = a + reach * (1 - 2 * up)
        j = b + near * (1 - 2 * along)
        fits = (reach >= 0) & (i >= 0) & (i < major) & (j >= 0) & (j < minor)
        fits = fits & ((reach > 0) | (up == 0)) & ((near > 0) | (along == 0))
        return fits, i, j

    def one_shard(turn, carry):
        fits, i, j = place_of(turn)

        @pl.when(fits & (far_from(i, j)))
        def _():
            slot = i * minor + j
            for piece in range(2):
                pltpu.make_async_copy(
                    held.at[slot, piece], held.at[slot, piece], recv_sem.at[slot, piece]
                ).wait()
                send_on(slot, piece, i, j)
            attend(slot, False)

        return carry

    def far_from(i, j):
        return (i != a) | (j != b)

    lax.fori_loop(1, rounds, one_shard, 0)

    per_peer = blocks_here // tp_size
    wide = kv_local * width

    def finish(query_block, h, put):
        at = pl.ds(pl.multiple_of(query_block * BLOCK_TOKENS, BLOCK_TOKENS), BLOCK_TOKENS)
        for g in range(groups):
            lanes = pl.ds(g * BLOCK_TOKENS, BLOCK_TOKENS)
            bottom = weight_sum[query_block, h, :, lanes]
            normed = (total[query_block, h, :, lanes] * (1.0 / bottom)).astype(jnp.bfloat16)
            put(h * groups + g, jnp.transpose(normed))
            log_norm[pl.ds(h * groups + g, 1), at] = (
                peak[query_block, h, :, lanes] * factor + jnp.log(bottom)
            )

    swaps = []
    for turn in range(1, tp_size + 1):
        peer = (mine + turn) % tp_size
        for k in range(per_peer):
            query_block = peer * per_peer + k
            out_rows = pl.ds(k * BLOCK_TOKENS, BLOCK_TOKENS)
            for h in range(kv_local):
                if turn < tp_size:

                    def put(head, tile, query_block=query_block):
                        leaving[query_block, :, pl.ds(head * HEAD_SIZE, HEAD_SIZE)] = tile

                else:

                    def put(head, tile, out_rows=out_rows):
                        at = pl.multiple_of(mine * wide + head * HEAD_SIZE, HEAD_SIZE)
                        attended[out_rows, pl.ds(at, HEAD_SIZE)] = tile

                finish(query_block, h, put)
                if turn < tp_size:
                    source = pl.ds(h * width, width)
                    target = pl.ds(pl.multiple_of(mine * wide + h * width, HEAD_SIZE), width)
                    copy = pltpu.make_async_remote_copy(
                        src_ref=leaving.at[query_block, :, source],
                        dst_ref=attended.at[out_rows, target],
                        send_sem=swap_send.at[turn - 1, k, h],
                        recv_sem=swap_recv.at[turn - 1, k, h],
                        device_id={"tp": peer},
                        device_id_type=MESH,
                    )
                    copy.start()
                    swaps.append(copy)

    def settle(turn, carry):
        fits, i, j = place_of(turn)

        @pl.when(fits)
        def _():
            slot = i * minor + j
            for piece in range(2):
                for wanted, copy in onward(slot, piece, i, j):

                    @pl.when(wanted)
                    def _(copy=copy):
                        copy.wait_send()

        return carry

    lax.fori_loop(0, rounds, settle, 0)
    for copy in swaps:
        copy.wait()


def body(tp_size, ctx_size, queries, rotated_key_rows, ordered_value_rows, block_order, live_blocks):
    tok_rows, own_columns = queries.shape
    kv_columns = rotated_key_rows.shape[1]
    kv_local = kv_columns // HEAD_SIZE
    heads_local = own_columns // HEAD_SIZE
    groups = heads_local // kv_local
    blocks_here = tok_rows // BLOCK_TOKENS
    width = groups * BLOCK_TOKENS
    major, minor = grid_of(ctx_size)
    dims = (major, minor, tp_size, kv_local, groups, blocks_here, live_blocks.shape[1])
    per_peer = blocks_here // tp_size
    whole = pl.BlockSpec(memory_space=pltpu.VMEM)
    small = pl.BlockSpec(memory_space=pltpu.SMEM)
    apart = pl.BlockSpec(memory_space=pl.ANY)
    results = pl.pallas_call(
        functools.partial(kernel, dims),
        out_shape=(
            pltpu.VMEM((tok_rows // tp_size, own_columns * tp_size), jnp.bfloat16),
            pltpu.VMEM((heads_local, tok_rows), jnp.float32),
        ),
        in_specs=[apart, apart, apart, small, small],
        out_specs=(whole, whole),
        scratch_shapes=[
            pltpu.VMEM((ctx_size, 2, tok_rows, kv_columns), jnp.bfloat16),
            pltpu.VMEM((tok_rows, own_columns), jnp.bfloat16),
            pltpu.VMEM((blocks_here, kv_local, HEAD_SIZE, width), jnp.bfloat16),
            pltpu.VMEM((blocks_here, kv_local, HEAD_SIZE, width), jnp.float32),
            pltpu.VMEM((blocks_here, kv_local, 1, width), jnp.float32),
            pltpu.VMEM((blocks_here, kv_local, 1, width), jnp.float32),
            pltpu.VMEM((blocks_here, BLOCK_TOKENS, own_columns), jnp.bfloat16),
            pltpu.SMEM((2, blocks_here * blocks_here), jnp.float32),
            pltpu.VMEM((SLOTS, tok_rows, CHUNK), jnp.float32),
            pltpu.SemaphoreType.DMA((3,)),
            pltpu.SemaphoreType.DMA((ctx_size, 2, 4)),
            pltpu.SemaphoreType.DMA((ctx_size, 2)),
            pltpu.SemaphoreType.DMA((tp_size - 1, per_peer, kv_local)),
            pltpu.SemaphoreType.DMA((tp_size - 1, per_peer, kv_local)),
        ],
        compiler_params=pltpu.CompilerParams(collective_id=0, has_side_effects=True),
        name="gather_attend",
    )(queries, rotated_key_rows, ordered_value_rows, block_order.reshape(1, -1), live_blocks)
    return results


def solution(mesh):
    placed = (
        P(("rep", "ctx"), "tp"),
        P(("rep", "ctx"), "tp"),
        P(("rep", "ctx"), "tp"),
        P("rep"),
        P("rep", None),
    )
    return jax.shard_map(
        functools.partial(body, mesh.shape["tp"], mesh.shape["ctx"]),
        mesh=mesh,
        in_specs=placed,
        out_specs=(P(("rep", "ctx", "tp"), None), P(("rep", "tp"), "ctx")),
        check_vma=False,
    )
```
